32 devices in a mesh: grp: 4 (over x, core), row: 8 (over z, y).
Axes of the slice: x: 2, y: 2, z: 4, core: 2. Of those that a mesh axis runs over, the one named last changes fastest.
Arguments:
- table: float32 [8, 65536, 128], P('grp', 'row'), may hold values from -6 to 6
- row_shard: int32 [8, 8192, 1], P('grp'), may hold values from 0 to 7; in each aligned block of 256 rows (0 to 255, 256 to 511, ..., all dimensions but the last counted through in order) at most 96 rows name the same one
- row_offset: int32 [8, 8192], P('grp'), may hold values from 0 to 8191
- bag_lengths: int32 [8, 32, 128], P('grp'), may hold values from 1 to 4, 256 in all within a row
Outputs:
- pooled: float32 [8, 4096, 128], P(None, ('grp', 'row'))
The draws below stay inside these ranges and needn't reach their ends.
Inputs may be any that keep to these rules, and one draw needn't show every extreme that they name: `row_shard`: in each aligned block of 256 lookups of a table (the lookups of one block of bags), at most 96 lookups name the same row shard, and in every draw some block reaches 96. `bag_lengths`: the 128 lengths of each block sum to 256.
All inputs are finite; a program needn't handle non-finite values.
Results may differ from the reference program's by a relative error of at most 0.0003.
Values sent between devices are 32-bit elements; how exact they have to be, the bound alone decides.
A program may use at most 64 MiB of HBM per device.

```python
import math
import jax
import jax.numpy as jnp
import numpy as np
from jax import lax

E = 128
POOL = 2
BAGS_BLK = 128
ROWS_DEV = 8192
TABLES = 8
BLOCKS = 32
BAGS = 4096
LOOK_BLK = 256
LOOKUPS = 8192
ROWS = 65536
CAP = 96
N_ROW = 8


def place_ends(array, key, low, high):
    place = [jax.random.randint(jax.random.fold_in(key, axis), (), 0, length) for axis, length in enumerate(array.shape)]
    main_axis = array.shape.index(max(array.shape))
    neighbour = place[:main_axis] + [(place[main_axis] + 1) % array.shape[main_axis]] + place[main_axis + 1:]
    return array.at[tuple(place)].set(low).at[tuple(neighbour)].set(high)


def block_scale(own_key, shape, cuts, smallest, high):
    def one(axis_at, parts):
        steps = jax.random.uniform(jax.random.fold_in(jax.random.fold_in(own_key, 6), axis_at), (parts,), jnp.float32, smallest / len(cuts), high / len(cuts))
        return jnp.repeat(jnp.exp(steps), shape[axis_at] // parts).reshape((-1,) + (1,) * (len(shape) - axis_at - 1))

    gain = one(*cuts[0])
    for cut in cuts[1:]:
        gain = gain * one(*cut)
    return gain


def split_up(number_of, total, bound, lean):
    weights = [(1 << 20) // math.isqrt(grade ** lean) + 1 for grade in range(2, number_of + 1)]
    rest, given = total - bound - (number_of - 1), [1] * (number_of - 1)
    while rest > 0:
        movable = [i for i in range(number_of - 1) if given[i] < bound]
        whole, left = sum([weights[i] for i in movable]), rest
        for i in movable:
            extra = min(bound - given[i], max(1, left * weights[i] // whole), rest)
            given[i] = given[i] + extra
            rest = rest - extra
    return np.array([bound] + given)


def ragged(own_key, amount, total, bound, slope):
    if amount == 2:
        one = jax.random.randint(own_key, (), max(1, total - bound), min(bound, total - 1) + 1)
        return jnp.stack([one, total - one])
    sizes = jnp.asarray(split_up(amount, total, bound, slope), jnp.int32)
    pairs = (amount - 1) // 2
    source_of, sink = sizes[1:1 + 2 * pairs:2], sizes[2:2 + 2 * pairs:2]
    margin = jnp.minimum(source_of - 1, bound - sink)
    shifted = jax.random.randint(jax.random.fold_in(own_key, 1), (pairs,), 0, 1 << 20) % (margin + 1)
    sizes = sizes.at[1:1 + 2 * pairs:2].set(source_of - shifted).at[2:2 + 2 * pairs:2].set(sink + shifted)
    return sizes[jax.random.permutation(jax.random.fold_in(own_key, 2), amount)]


def assign_block(stream_key, own, number, rows, amount, top, reach, skew):
    ranking = jax.random.permutation(stream_key, amount)
    crowded, ordinary = load_shares(amount, rows * top, reach, skew, True), load_shares(amount, rows * top, reach, skew, False)
    places = jnp.arange(amount)

    def named(sizes, offset_by):
        used = int((sizes > 0).sum())
        fixed = max(1, used // 4)
        passed = fixed + (places - fixed + offset_by * (used - fixed)) % max(1, amount - fixed)
        return jnp.zeros((amount,), jnp.int32).at[ranking[jnp.where(places < fixed, places, passed)]].set(jnp.asarray(sizes, jnp.int32))

    sizes = jnp.where(number % 4 == 0, named(crowded, number // 4), named(ordinary, number - number // 4 - 1))
    mixed = jax.random.permutation(jax.random.fold_in(own, 3), amount)
    source_of, receiver = mixed[0:amount // 2 * 2:2], mixed[1:amount // 2 * 2:2]
    slack = jnp.minimum(sizes[source_of] - 1, reach - sizes[receiver]) // 2
    slack = jnp.where((source_of == ranking[0]) | (receiver == ranking[0]) | (sizes[receiver] == 0), 0, jnp.maximum(slack, 0))
    passed = jax.random.randint(jax.random.fold_in(own, 4), (amount // 2,), 0, 1 << 20) % (slack + 1)
    sizes = sizes.at[source_of].add(-passed).at[receiver].add(passed)
    members = jnp.searchsorted(jnp.cumsum(sizes), jnp.arange(rows * top), side="right").astype(jnp.int32)
    grid = members.reshape(top, rows).T
    grid = grid[jax.random.permutation(jax.random.fold_in(own, 1), rows)]
    offset_by = jax.random.randint(jax.random.fold_in(own, 2), (rows, 1), 0, top)
    return jnp.take_along_axis(grid, (jnp.arange(top)[None, :] + offset_by) % top, axis=1)


def load_shares(count, total, reach, skew, full):
    portions = [(1 << 20) // math.isqrt(standing ** skew) + 1 for standing in range(1, count + 1)]
    largest = reach if full else min(reach, max(-(-total // count), total * portions[0] // sum(portions)))
    least = 1 if total - largest >= count - 1 else 0
    given, rest = [largest] + [least] * (count - 1), total - largest - least * (count - 1)
    while rest > 0:
        free = [i for i in range(1, count) if given[i] < largest] or [i for i in range(1, count) if given[i] < reach]
        pool, left = sum([portions[i] for i in free]), rest
        for i in free:
            addition = min(reach - given[i], max(1, left * portions[i] // pool), rest)
            given[i] = given[i] + addition
            rest = rest - addition
    return np.array(given)


def bell_draw(rng, extent, width, bound, split=(), held_as=jnp.bfloat16):
    values = jax.random.normal(rng, extent, jnp.float32) * width
    if len(split) > 0:
        values = block_scale(rng, extent, split, -0.22, 0.18) * values
    return jnp.clip(values, min=-bound, max=bound).astype(held_as)


def setup_inputs(seed: int = 0) -> dict:
    streams_of = jax.random.split(jax.random.key(seed), 5)
    table = bell_draw(streams_of[0], (TABLES, ROWS, E), 1.0, 6.0, ((0, 4), (1, 8)), jnp.float32)
    row_shard_keys = jax.random.split(jax.random.fold_in(streams_of[1], 1), TABLES * LOOKUPS // LOOK_BLK)
    row_shard_turns = jax.random.permutation(jax.random.fold_in(streams_of[1], 3), TABLES * LOOKUPS // LOOK_BLK)
    row_shard = jax.vmap(lambda own, number: assign_block(jax.random.fold_in(streams_of[1], 2), own, number, LOOK_BLK, N_ROW, 1, CAP, 2))(row_shard_keys, row_shard_turns).reshape((TABLES, LOOKUPS, 1))
    row_offset = place_ends(jax.random.randint(streams_of[2], (TABLES, LOOKUPS), 0, ROWS_DEV), jax.random.fold_in(streams_of[2], 1), 0, ROWS_DEV - 1).astype(jnp.int32)
    bag_lengths = jax.vmap(lambda own: ragged(own, BAGS_BLK, LOOK_BLK, 2 * POOL, 1))(jax.random.split(streams_of[3], TABLES * BLOCKS)).reshape((TABLES, BLOCKS, BAGS_BLK)).astype(jnp.int32)
    return dict(table=table, row_shard=row_shard, row_offset=row_offset, bag_lengths=bag_lengths)


def pool_one(packed):
    matrix, shard_ids, offsets, lengths = packed
    row_index = shard_ids[:, 0] * ROWS_DEV + offsets
    vectors = jnp.take(matrix, row_index, axis=0)
    ends = jnp.cumsum(lengths, axis=-1).astype(jnp.int32)
    places = jnp.arange(LOOK_BLK, dtype=jnp.int32)
    within = jnp.sum((ends[:, None, :] <= places[None, :, None]).astype(jnp.int32), axis=-1).astype(jnp.int32)
    bag_index = within + (jnp.arange(BLOCKS, dtype=jnp.int32) * BAGS_BLK)[:, None]
    return jax.ops.segment_sum(vectors, bag_index.reshape(-1), num_segments=BAGS)


def reference(table, row_shard, row_offset, bag_lengths):
    return lax.map(pool_one, (table, row_shard, row_offset, bag_lengths))
```

```python
import functools
import jax
import jax.numpy as jnp
from jax import lax
from jax.experimental import pallas as pl
from jax.experimental.pallas import tpu as pltpu
from jax.sharding import PartitionSpec as P

MESH = pl.DeviceIdType.MESH


def kernel(dims, off_ref, bag_ref, table_hbm, out_ref, *scratch):
    tables, groups, shards, cap, bags = dims
    held = scratch[:tables]
    (ysend, comb, part, fromleft, fromright,
     tab_sem, ys_sem, yr_sem, zs_sem, lr_sem, rr_sem, fs_sem, fr_sem, own_sem) = scratch[tables:]
    line = shards // 2
    g = lax.axis_index("grp")
    r = lax.axis_index("row")
    q = r // 2
    p = r % 2
    mate = q * 2 + 1 - p

    loads = [pltpu.make_async_copy(table_hbm.at[t], held[t], tab_sem.at[t]) for t in range(tables)]
    for load in loads:
        load.start()

    barrier = pltpu.get_barrier_semaphore()
    pl.semaphore_signal(barrier, inc=1, device_id=(g, mate), device_id_type=MESH)

    @pl.when(q > 0)
    def _():
        pl.semaphore_signal(barrier, inc=1, device_id=(g, r - 2), device_id_type=MESH)

    @pl.when(q < line - 1)
    def _():
        pl.semaphore_signal(barrier, inc=1, device_id=(g, r + 2), device_id_type=MESH)

    for step in range(1, groups):
        pl.semaphore_signal(barrier, inc=1, device_id=((g + step) % groups, r), device_id_type=MESH)
    pl.semaphore_wait(barrier, groups + jnp.where(q > 0, 1, 0) + jnp.where(q < line - 1, 1, 0))

    def target(j):
        picked = 0
        for at in range(line):
            order = sorted(range(line), key=lambda d: (-abs(d - at), d))
            picked = picked + jnp.where(q == at, order[j], 0)
        return picked

    def ycopy(c):
        return pltpu.make_async_remote_copy(
            src_ref=ysend.at[c], dst_ref=comb.at[c, :, 1], send_sem=ys_sem.at[c], recv_sem=yr_sem.at[c],
            device_id=(g, mate), device_id_type=MESH)

    def rightcopy(c):
        return pltpu.make_async_remote_copy(
            src_ref=part.at[c], dst_ref=fromleft.at[c], send_sem=zs_sem.at[c], recv_sem=lr_sem.at[c],
            device_id=(g, r + 2), device_id_type=MESH)

    def leftcopy(c):
        return pltpu.make_async_remote_copy(
            src_ref=part.at[c], dst_ref=fromright.at[c], send_sem=zs_sem.at[c], recv_sem=rr_sem.at[c],
            device_id=(g, r - 2), device_id_type=MESH)

    def fcopy(c, t, step, towards):
        other = (g + towards * step + groups) % groups
        slot = t * groups + step
        return pltpu.make_async_remote_copy(
            src_ref=part.at[c, other], dst_ref=out_ref.at[g * tables + t], send_sem=fs_sem.at[slot],
            recv_sem=fr_sem.at[slot], device_id=(other, r), device_id_type=MESH)

    def gather(table, dst, base):
        @pl.loop(0, cap // 8)
        def _(i):
            for u in range(8):
                row = off_ref[base + i * 8 + u]
                dst[pl.ds(i * 8 + u, 1), :] = table[pl.ds(row, 1), :]

    def block(t, k, to, side):
        return ((t * groups + k) * line + to) * 2 + side

    def fetch(j, t):
        to = target(j)
        c = to * tables + t

        @pl.loop(0, groups)
        def _(k):
            gather(held[t], ysend.at[c, k], block(t, k, to, 1 - p) * cap)
        ycopy(c).start()

        @pl.loop(0, groups)
        def _(k):
            gather(held[t], comb.at[c, k, 0], block(t, k, to, p) * cap)

    def merge(j, t):
        to = target(j)
        c = to * tables + t
        ycopy(c).wait_recv()
        places = lax.broadcasted_iota(jnp.int32, (bags, 2 * cap), 0)

        @pl.loop(0, groups)
        def _(k):
            spot = (t * groups + k) * line + to
            weights = jnp.where(places == bag_ref[pl.ds(spot, 1), :], 1.0, 0.0).astype(jnp.bfloat16)
            vectors = jnp.concatenate([comb[c, k, 0], comb[c, k, 1]], axis=0)
            high = vectors.astype(jnp.bfloat16)
            low = (vectors - high.astype(jnp.float32)).astype(jnp.bfloat16)
            part[c, k] = (jnp.dot(weights, high, preferred_element_type=jnp.float32)
                          + jnp.dot(weights, low, preferred_element_type=jnp.float32))

        def add(buffer):
            @pl.loop(0, groups)
            def _(k):
                part[c, k] = part[c, k] + buffer[c, k]

        @pl.when(jnp.logical_and(to >= q, q > 0))
        def _():
            rightcopy(c).wait_recv()
            add(fromleft)

        @pl.when(jnp.logical_and(to <= q, q < line - 1))
        def _():
            leftcopy(c).wait_recv()
            add(fromright)

        if j < line - 1:
            @pl.when(to > q)
            def _():
                rightcopy(c).start()

            @pl.when(to < q)
            def _():
                leftcopy(c).start()
        else:
            for step in range(1, groups):
                fcopy(c, t, step, 1).start()
            pltpu.make_async_copy(part.at[c, g], out_ref.at[g * tables + t], own_sem.at[t]).start()

    items = [(j, t) for j in range(line) for t in range(tables)]
    for n, (j, t) in enumerate(items):
        if n < tables:
            loads[t].wait()
        fetch(j, t)
        if n > 0:
            merge(*items[n - 1])
    merge(*items[-1])

    for j, t in items:
        to = target(j)
        c = to * tables + t
        ycopy(c).wait_send()
        if j < line - 1:
            rightcopy(c).wait_send()
    for t in range(tables):
        c = q * tables + t
        pltpu.make_async_copy(part.at[c, g], out_ref.at[g * tables + t], own_sem.at[t]).wait()
        for step in range(1, groups):
            fcopy(c, t, step, 1).wait_send()
            origin = (g - step + groups) % groups
            slot = t * groups + step
            pltpu.make_async_remote_copy(
                src_ref=part.at[c, g], dst_ref=out_ref.at[origin * tables + t], send_sem=fs_sem.at[slot],
                recv_sem=fr_sem.at[slot], device_id=(origin, r), device_id_type=MESH).wait_recv()


def body(table, row_shard, row_offset, bag_lengths):
    groups = lax.axis_size("grp")
    shards = lax.axis_size("row")
    line = shards // 2
    mine = lax.axis_index("row")
    side = mine % 2
    tables, rows, width = table.shape
    bags = bag_lengths.shape[2]
    look = row_offset.shape[1] // (groups * shards)
    cap = 3 * look // shards
    blocks = groups * shards
    owner = row_shard.reshape(tables * blocks, look)
    offset = row_offset.reshape(tables * blocks, look)
    before = jnp.triu(jnp.ones((look, look), jnp.bfloat16), 1)

    def ranks(owners, shard):
        local = owners == shard
        rank = jnp.dot(local.astype(jnp.bfloat16), before, preferred_element_type=jnp.float32).astype(jnp.int32)
        return jnp.where(local, rank, -1)

    def pack(rank, values):
        slots = lax.broadcasted_iota(jnp.int32, (1, cap, 1), 1)
        return jnp.sum(jnp.where(rank[:, None, :] == slots, values[:, None, :], 0), axis=2)

    packed_offset = pack(ranks(owner, mine), offset)
    near = lax.dynamic_index_in_dim(owner.reshape(tables * groups * line, 2, look), side, 1, keepdims=False)
    lengths = lax.dynamic_index_in_dim(bag_lengths.reshape(tables * groups * line, 2, bags), side, 1, keepdims=False)
    upto = jnp.triu(jnp.ones((bags, bags), jnp.bfloat16))
    ends = jnp.dot(lengths.astype(jnp.bfloat16), upto, preferred_element_type=jnp.float32).astype(jnp.int32)
    places = lax.broadcasted_iota(jnp.int32, (1, 1, look), 2)
    within = jnp.sum((ends[:, :, None] <= places).astype(jnp.int32), axis=1)
    mate = mine + 1 - 2 * side
    packed_bag = jnp.concatenate([pack(ranks(near, mine), within + 1), pack(ranks(near, mate), within + 1)], axis=1) - 1

    chunks = line * tables
    dims = (tables, groups, shards, cap, bags)
    return pl.pallas_call(
        functools.partial(kernel, dims),
        out_shape=jax.ShapeDtypeStruct((groups * tables, bags, width), jnp.float32),
        in_specs=[pl.BlockSpec(memory_space=pltpu.SMEM), pl.BlockSpec(memory_space=pltpu.VMEM), pl.BlockSpec(memory_space=pl.ANY)],
        out_specs=pl.BlockSpec(memory_space=pltpu.VMEM),
        scratch_shapes=[
            *[pltpu.VMEM((rows, width), jnp.float32) for _ in range(tables)],
            pltpu.VMEM((chunks, groups, cap, width), jnp.float32),
            pltpu.VMEM((chunks, groups, 2, cap, width), jnp.float32),
            pltpu.VMEM((chunks, groups, bags, width), jnp.float32),
            pltpu.VMEM((chunks, groups, bags, width), jnp.float32),
            pltpu.VMEM((chunks, groups, bags, width), jnp.float32),
            pltpu.SemaphoreType.DMA((tables,)),
            pltpu.SemaphoreType.DMA((chunks,)),
            pltpu.SemaphoreType.DMA((chunks,)),
            pltpu.SemaphoreType.DMA((chunks,)),
            pltpu.SemaphoreType.DMA((chunks,)),
            pltpu.SemaphoreType.DMA((chunks,)),
            pltpu.SemaphoreType.DMA((tables * groups,)),
            pltpu.SemaphoreType.DMA((tables * groups,)),
            pltpu.SemaphoreType.DMA((tables,)),
        ],
        compiler_params=pltpu.CompilerParams(collective_id=0, has_side_effects=True, vmem_limit_bytes=63 * 2**20),
    )(packed_offset.reshape(-1), packed_bag, table)


def solution(mesh):
    placed = (P("grp", "row", None), P("grp", None, None), P("grp", None), P("grp", None, None))
    return jax.shard_map(
        body, mesh=mesh, in_specs=placed, out_specs=P(None, ("grp", "row"), None), check_vma=False
    )
```

```python
import functools
import jax
import jax.numpy as jnp
from jax import lax
from jax.experimental import pallas as pl
from jax.experimental.pallas import tpu as pltpu
from jax.sharding import PartitionSpec as P

MESH = pl.DeviceIdType.MESH


def kernel(dims, off_ref, bag_ref, table, out_ref, ysend, comb, part, fromleft, fromright,
           ys_sem, yr_sem, zs_sem, lr_sem, rr_sem, fs_sem, fr_sem, own_sem):
    tables, groups, shards, cap, bags = dims
    line = shards // 2
    chips = groups // 2
    pieces = line * groups
    ahead = min(4, pieces)
    g = lax.axis_index("grp")
    r = lax.axis_index("row")
    q = r // 2
    p = r % 2
    mate = q * 2 + 1 - p

    barrier = pltpu.get_barrier_semaphore()
    pl.semaphore_signal(barrier, inc=1, device_id=(g, mate), device_id_type=MESH)

    @pl.when(q > 0)
    def _():
        pl.semaphore_signal(barrier, inc=1, device_id=(g, r - 2), device_id_type=MESH)

    @pl.when(q < line - 1)
    def _():
        pl.semaphore_signal(barrier, inc=1, device_id=(g, r + 2), device_id_type=MESH)

    for step in range(1, groups):
        pl.semaphore_signal(barrier, inc=1, device_id=((g + step) % groups, r), device_id_type=MESH)
    pl.semaphore_wait(barrier, groups + jnp.where(q > 0, 1, 0) + jnp.where(q < line - 1, 1, 0))

    def target(j):
        picked = 0
        for at in range(line):
            order = sorted(range(line), key=lambda d: (-abs(d - at), d))
            for i in range(line):
                picked = picked + jnp.where(jnp.logical_and(q == at, j == i), order[i], 0)
        return picked

    def peer(s):
        return (g // 2 + s // 2) % chips * 2 + (g % 2 + s % 2) % 2

    def origin(s):
        return (g // 2 + chips - s // 2) % chips * 2 + (g % 2 + s % 2) % 2

    def place(n):
        to = target(n // groups)
        s = groups - 1 - n % groups
        return to, s, peer(s)

    def ycopy(c, k):
        return pltpu.make_async_remote_copy(
            src_ref=ysend.at[c, k], dst_ref=comb.at[c, k, 1], send_sem=ys_sem.at[c, k], recv_sem=yr_sem.at[c, k],
            device_id=(g, mate), device_id_type=MESH)

    def rightcopy(c, k):
        return pltpu.make_async_remote_copy(
            src_ref=part.at[c, k], dst_ref=fromleft.at[c, k], send_sem=zs_sem.at[c, k], recv_sem=lr_sem.at[c, k],
            device_id=(g, r + 2), device_id_type=MESH)

    def leftcopy(c, k):
        return pltpu.make_async_remote_copy(
            src_ref=part.at[c, k], dst_ref=fromright.at[c, k], send_sem=zs_sem.at[c, k], recv_sem=rr_sem.at[c, k],
            device_id=(g, r - 2), device_id_type=MESH)

    def ownercopy(c, t, s, k, home):
        return pltpu.make_async_remote_copy(
            src_ref=part.at[c, k], dst_ref=out_ref.at[home * tables + t], send_sem=fs_sem.at[t, s],
            recv_sem=fr_sem.at[t, s], device_id=(k, r), device_id_type=MESH)

    def homecopy(c, t):
        return pltpu.make_async_copy(part.at[c, g], out_ref.at[g * tables + t], own_sem.at[t])

    def gather(t, dst, base):
        @pl.loop(0, cap // 8)
        def _(i):
            for u in range(8):
                row = off_ref[base + i * 8 + u]
                dst[pl.ds(i * 8 + u, 1), :] = table[t, pl.ds(row, 1), :]

    def fetch(n):
        to, s, k = place(n)
        for t in range(tables):
            c = to * tables + t
            first = ((t * groups + k) * line + to) * 2
            gather(t, ysend.at[c, k], (first + 1 - p) * cap)
            ycopy(c, k).start()
        for t in range(tables):
            c = to * tables + t
            first = ((t * groups + k) * line + to) * 2
            gather(t, comb.at[c, k, 0], (first + p) * cap)

    def merge(n):
        to, s, k = place(n)
        places = lax.broadcasted_iota(jnp.int32, (bags, 2 * cap), 0)
        for t in range(tables):
            c = to * tables + t
            spot = (t * groups + k) * line + to
            ycopy(c, k).wait_recv()
            weights = jnp.where(places == bag_ref[pl.ds(spot, 1), :], 1.0, 0.0).astype(jnp.bfloat16)
            vectors = jnp.concatenate([comb[c, k, 0], comb[c, k, 1]], axis=0)
            high = vectors.astype(jnp.bfloat16)
            low = (vectors - high.astype(jnp.float32)).astype(jnp.bfloat16)
            part[c, k] = (jnp.dot(weights, high, preferred_element_type=jnp.float32)
                          + jnp.dot(weights, low, preferred_element_type=jnp.float32))

            @pl.when(jnp.logical_and(to >= q, q > 0))
            def _():
                rightcopy(c, k).wait_recv()
                part[c, k] = part[c, k] + fromleft[c, k]

            @pl.when(jnp.logical_and(to <= q, q < line - 1))
            def _():
                leftcopy(c, k).wait_recv()
                part[c, k] = part[c, k] + fromright[c, k]

            @pl.when(to > q)
            def _():
                rightcopy(c, k).start()

            @pl.when(to < q)
            def _():
                leftcopy(c, k).start()

            @pl.when(jnp.logical_and(to == q, s > 0))
            def _():
                ownercopy(c, t, s, k, g).start()

            @pl.when(jnp.logical_and(to == q, s == 0))
            def _():
                homecopy(c, t).start()

    @pl.loop(0, ahead)
    def _(n):
        fetch(n)

    @pl.loop(0, pieces - ahead)
    def _(n):
        fetch(n + ahead)
        merge(n)

    @pl.loop(pieces - ahead, pieces)
    def _(n):
        merge(n)

    @pl.loop(0, pieces)
    def _(n):
        to, s, k = place(n)
        for t in range(tables):
            c = to * tables + t
            ycopy(c, k).wait_send()

            @pl.when(to != q)
            def _():
                rightcopy(c, k).wait_send()

    @pl.loop(1, groups)
    def _(s):
        for t in range(tables):
            c = q * tables + t
            ownercopy(c, t, s, peer(s), g).wait_send()
            ownercopy(c, t, s, origin(s), origin(s)).wait_recv()

    for t in range(tables):
        homecopy(q * tables + t, t).wait()


def body(table, row_shard, row_offset, bag_lengths):
    groups = lax.axis_size("grp")
    shards = lax.axis_size("row")
    line = shards // 2
    mine = lax.axis_index("row")
    side = mine % 2
    tables, rows, width = table.shape
    bags = bag_lengths.shape[2]
    look = row_offset.shape[1] // (groups * shards)
    cap = 3 * look // shards
    blocks = groups * shards
    owner = row_shard.reshape(tables * blocks, look)
    offset = row_offset.reshape(tables * blocks, look)
    before = jnp.triu(jnp.ones((look, look), jnp.bfloat16), 1)

    def ranks(owners, shard):
        local = owners == shard
        rank = jnp.dot(local.astype(jnp.bfloat16), before, preferred_element_type=jnp.float32).astype(jnp.int32)
        return jnp.where(local, rank, -1)

    def pack(rank, values):
        slots = lax.broadcasted_iota(jnp.int32, (1, cap, 1), 1)
        return jnp.sum(jnp.where(rank[:, None, :] == slots, values[:, None, :], 0), axis=2)

    packed_offset = pack(ranks(owner, mine), offset)
    near = lax.dynamic_index_in_dim(owner.reshape(tables * groups * line, 2, look), side, 1, keepdims=False)
    lengths = lax.dynamic_index_in_dim(bag_lengths.reshape(tables * groups * line, 2, bags), side, 1, keepdims=False)
    upto = jnp.triu(jnp.ones((bags, bags), jnp.bfloat16))
    ends = jnp.dot(lengths.astype(jnp.bfloat16), upto, preferred_element_type=jnp.float32).astype(jnp.int32)
    places = lax.broadcasted_iota(jnp.int32, (1, 1, look), 2)
    within = jnp.sum((ends[:, :, None] <= places).astype(jnp.int32), axis=1)
    mate = mine + 1 - 2 * side
    packed_bag = jnp.concatenate([pack(ranks(near, mine), within + 1), pack(ranks(near, mate), within + 1)], axis=1) - 1

    chunks = line * tables
    dims = (tables, groups, shards, cap, bags)
    return pl.pallas_call(
        functools.partial(kernel, dims),
        out_shape=jax.ShapeDtypeStruct((groups * tables, bags, width), jnp.float32),
        in_specs=[pl.BlockSpec(memory_space=pltpu.SMEM), pl.BlockSpec(memory_space=pltpu.VMEM), pl.BlockSpec(memory_space=pltpu.VMEM)],
        out_specs=pl.BlockSpec(memory_space=pltpu.VMEM),
        scratch_shapes=[
            pltpu.VMEM((chunks, groups, cap, width), jnp.float32),
            pltpu.VMEM((chunks, groups, 2, cap, width), jnp.float32),
            pltpu.VMEM((chunks, groups, bags, width), jnp.float32),
            pltpu.VMEM((chunks, groups, bags, width), jnp.float32),
            pltpu.VMEM((chunks, groups, bags, width), jnp.float32),
            *[pltpu.SemaphoreType.DMA((chunks, groups)) for _ in range(5)],
            pltpu.SemaphoreType.DMA((tables, groups)),
            pltpu.SemaphoreType.DMA((tables, groups)),
            pltpu.SemaphoreType.DMA((tables,)),
        ],
        compiler_params=pltpu.CompilerParams(collective_id=0, has_side_effects=True, vmem_limit_bytes=63 * 2**20),
    )(packed_offset.reshape(-1), packed_bag, table)


def solution(mesh):
    placed = (P("grp", "row", None), P("grp", None, None), P("grp", None), P("grp", None, None))
    return jax.shard_map(
        body, mesh=mesh, in_specs=placed, out_specs=P(None, ("grp", "row"), None), check_vma=False
    )
```

```python
import functools
import jax
import jax.numpy as jnp
from jax import lax
from jax.experimental import pallas as pl
from jax.experimental.pallas import tpu as pltpu
from jax.sharding import PartitionSpec as P

MESH = pl.DeviceIdType.MESH


def kernel(dims, shard_ref, offset_ref, length_ref, table_hbm, out_ref, *scratch):
    tables, groups, shards, cap, bags, look = dims
    held = scratch[:tables]
    (ysend, comb, part, fromleft, fromright, weights_of, staged, off_ref, earlier, starts_of, ends_of,
     ys_sem, yr_sem, zs_sem, lr_sem, rr_sem, fs_sem, fr_sem, own_sem, tab_sem, off_sem) = scratch[tables:]
    lanes = shard_ref.shape[1]
    halves = look // lanes
    blocks = groups * shards
    slots = weights_of.shape[0]
    line = shards // 2
    chips = groups // 2
    pieces = line * groups
    ahead = weights_of.shape[0] - 3
    g = lax.axis_index("grp")
    r = lax.axis_index("row")
    q = r // 2
    p = r % 2
    mate = q * 2 + 1 - p

    loads = [pltpu.make_async_copy(table_hbm.at[t], held[t], tab_sem.at[t]) for t in range(tables)]
    for load in loads:
        load.start()

    barrier = pltpu.get_barrier_semaphore()
    pl.semaphore_signal(barrier, inc=1, device_id=(g, mate), device_id_type=MESH)

    @pl.when(q > 0)
    def _():
        pl.semaphore_signal(barrier, inc=1, device_id=(g, r - 2), device_id_type=MESH)

    @pl.when(q < line - 1)
    def _():
        pl.semaphore_signal(barrier, inc=1, device_id=(g, r + 2), device_id_type=MESH)

    for step in range(1, groups):
        pl.semaphore_signal(barrier, inc=1, device_id=((g + step) % groups, r), device_id_type=MESH)

    def ones_where(keep):
        return jnp.where(keep, 1.0, 0.0).astype(jnp.bfloat16)

    def grid_of(size):
        return [lax.broadcasted_iota(jnp.int32, (size, size), axis) for axis in range(2)]

    down, across = grid_of(look)
    earlier[...] = ones_where(down < across)
    down, across = grid_of(bags)
    starts_of[...] = ones_where(across < down)
    ends_of[...] = ones_where(across <= down)

    def target(j):
        picked = 0
        for at in range(line):
            order = sorted(range(line), key=lambda d: (-abs(d - at), d))
            for i in range(line):
                picked = picked + jnp.where(jnp.logical_and(q == at, j == i), order[i], 0)
        return picked

    def peer(s):
        return (g // 2 + s // 2) % chips * 2 + (g % 2 + s % 2) % 2

    def origin(s):
        return (g // 2 + chips - s // 2) % chips * 2 + (g % 2 + s % 2) % 2

    def place(n):
        to = target(n // groups)
        s = groups - 1 - n % groups
        return to, s, peer(s)

    def ycopy(c, k):
        return pltpu.make_async_remote_copy(
            src_ref=ysend.at[c, k], dst_ref=comb.at[c, k, 1], send_sem=ys_sem.at[c, k], recv_sem=yr_sem.at[c, k],
            device_id=(g, mate), device_id_type=MESH)

    def rightcopy(c, k):
        return pltpu.make_async_remote_copy(
            src_ref=part.at[c, k], dst_ref=fromleft.at[c, k], send_sem=zs_sem.at[c, k], recv_sem=lr_sem.at[c, k],
            device_id=(g, r + 2), device_id_type=MESH)

    def leftcopy(c, k):
        return pltpu.make_async_remote_copy(
            src_ref=part.at[c, k], dst_ref=fromright.at[c, k], send_sem=zs_sem.at[c, k], recv_sem=rr_sem.at[c, k],
            device_id=(g, r - 2), device_id_type=MESH)

    def ownercopy(c, t, s, k, home):
        return pltpu.make_async_remote_copy(
            src_ref=part.at[c, k], dst_ref=out_ref.at[home * tables + t], send_sem=fs_sem.at[t, s],
            recv_sem=fr_sem.at[t, s], device_id=(k, r), device_id_type=MESH)

    def homecopy(c, t):
        return pltpu.make_async_copy(part.at[c, g], out_ref.at[g * tables + t], own_sem.at[t])

    def across_lanes(a, b):
        return lax.dot_general(a, b, (((1,), (1,)), ((), ())), preferred_element_type=jnp.float32)

    def shards_at(t, o):
        return jnp.concatenate([shard_ref[pl.ds((t * blocks + o) * halves + h, 1), :] for h in range(halves)], axis=1)

    def offsets_at(t, o):
        return jnp.concatenate([offset_ref[pl.ds((o * halves + h) * tables + t, 1), :] for h in range(halves)], axis=1)

    def prepare(n):
        to, s, k = place(n)
        slot = n % slots
        away, here = (k * line + to) * 2 + 1 - p, (k * line + to) * 2 + p
        local = []
        for t in range(tables):
            local.append(jnp.where(shards_at(t, away) == r, 1.0, 0.0))
            local.append(jnp.where(shards_at(t, here) == r, 1.0, 0.0))
            local.append(jnp.where(shards_at(t, here) == mate, 1.0, 0.0))
        local += [jnp.zeros_like(local[0])] * (-len(local) % 8)
        local = jnp.concatenate(local, axis=0)
        rank = jnp.dot(local.astype(jnp.bfloat16), earlier[...], preferred_element_type=jnp.float32)
        rank = jnp.where(local > 0.5, rank, -1.0).astype(jnp.int32)
        slot_ids = lax.broadcasted_iota(jnp.int32, (cap, look), 0)
        places = lax.broadcasted_iota(jnp.int32, (bags, look), 1).astype(jnp.float32)
        for t in range(tables):
            sent, kept, given = [ones_where(rank[3 * t + i:3 * t + i + 1, :] == slot_ids) for i in range(3)]
            for i, (o, chosen) in enumerate(((away, sent), (here, kept))):
                wanted = offsets_at(t, o)
                digits = [wanted // 128, wanted % 128] + [jnp.zeros_like(wanted)] * 6
                digits = jnp.concatenate(digits, axis=0).astype(jnp.float32).astype(jnp.bfloat16)
                packed = across_lanes(digits, chosen)
                index = packed[0:1, :] * 128.0 + packed[1:2, :]
                index = jnp.clip(index.astype(jnp.int32), 0, held[t].shape[0] - 1)
                staged[slot, pl.ds(2 * t + i, 1), pl.ds(0, cap)] = index
            lengths = length_ref[pl.ds(t * blocks + here, 1), :].astype(jnp.float32)
            lengths = jnp.broadcast_to(lengths, (8, bags)).astype(jnp.bfloat16)
            starts = across_lanes(starts_of[...], lengths)[:, 0:1]
            ends = across_lanes(ends_of[...], lengths)[:, 0:1]
            member = ones_where(jnp.logical_and(places >= starts, places < ends))
            weights = across_lanes(member, jnp.concatenate([kept, given], axis=0))
            weights_of[slot, t] = weights.astype(jnp.bfloat16)

    def toscalars(n):
        slot = n % slots
        return pltpu.make_async_copy(staged.at[slot], off_ref.at[slot], off_sem.at[slot])

    def gather(slot, t, i, dst):
        @pl.loop(0, cap // 8)
        def _(b):
            for u in range(8):
                row = off_ref[slot, 2 * t + i, b * 8 + u]
                dst[pl.ds(b * 8 + u, 1), :] = held[t][pl.ds(row, 1), :]

    def fetch(n):
        to, s, k = place(n)
        slot = n % slots
        toscalars(n).wait()
        for t in range(tables):
            c = to * tables + t
            gather(slot, t, 0, ysend.at[c, k])
            ycopy(c, k).start()
        for t in range(tables):
            gather(slot, t, 1, comb.at[to * tables + t, k, 0])

    def merge(n):
        to, s, k = place(n)
        for t in range(tables):
            c = to * tables + t
            ycopy(c, k).wait_recv()
            weights = weights_of[n % slots, t]
            vectors = jnp.concatenate([comb[c, k, 0], comb[c, k, 1]], axis=0)
            high = vectors.astype(jnp.bfloat16)
            low = (vectors - high.astype(jnp.float32)).astype(jnp.bfloat16)
            part[c, k] = (jnp.dot(weights, high, preferred_element_type=jnp.float32)
                          + jnp.dot(weights, low, preferred_element_type=jnp.float32))

            @pl.when(jnp.logical_and(to >= q, q > 0))
            def _():
                rightcopy(c, k).wait_recv()
                part[c, k] = part[c, k] + fromleft[c, k]

            @pl.when(jnp.logical_and(to <= q, q < line - 1))
            def _():
                leftcopy(c, k).wait_recv()
                part[c, k] = part[c, k] + fromright[c, k]

            @pl.when(to > q)
            def _():
                rightcopy(c, k).start()

            @pl.when(to < q)
            def _():
                leftcopy(c, k).start()

            @pl.when(jnp.logical_and(to == q, s > 0))
            def _():
                ownercopy(c, t, s, k, g).start()

            @pl.when(jnp.logical_and(to == q, s == 0))
            def _():
                homecopy(c, t).start()

    prepare(0)
    prepare(1)
    toscalars(0).start()
    for load in loads:
        load.wait()
    pl.semaphore_wait(barrier, groups + jnp.where(q > 0, 1, 0) + jnp.where(q < line - 1, 1, 0))

    @pl.loop(2, pieces + ahead + 2)
    def _(m):
        @pl.when(m - 2 < pieces)
        def _():
            fetch(m - 2)

        @pl.when(m - 1 < pieces)
        def _():
            toscalars(m - 1).start()

        @pl.when(m < pieces)
        def _():
            prepare(m)

        @pl.when(m - 2 - ahead >= 0)
        def _():
            merge(m - 2 - ahead)

    @pl.loop(0, pieces)
    def _(n):
        to, s, k = place(n)
        for t in range(tables):
            c = to * tables + t
            ycopy(c, k).wait_send()

            @pl.when(to != q)
            def _():
                rightcopy(c, k).wait_send()

    @pl.loop(1, groups)
    def _(s):
        for t in range(tables):
            c = q * tables + t
            ownercopy(c, t, s, peer(s), g).wait_send()
            ownercopy(c, t, s, origin(s), origin(s)).wait_recv()

    for t in range(tables):
        homecopy(q * tables + t, t).wait()


def body(table, row_shard, row_offset, bag_lengths):
    groups = lax.axis_size("grp")
    shards = lax.axis_size("row")
    line = shards // 2
    tables, rows, width = table.shape
    bags = bag_lengths.shape[2]
    blocks = groups * shards
    look = row_offset.shape[1] // blocks
    cap = 3 * look // shards
    lanes = min(look, 128)
    strips = row_offset.shape[1] // lanes
    chunks = line * tables
    slots = 7
    held_rows = -(-2 * tables // 8) * 8
    dims = (tables, groups, shards, cap, bags, look)
    vector, dma = pltpu.VMEM, pltpu.SemaphoreType.DMA
    in_vmem = pl.BlockSpec(memory_space=pltpu.VMEM)
    return pl.pallas_call(
        functools.partial(kernel, dims),
        out_shape=jax.ShapeDtypeStruct((groups * tables, bags, width), jnp.float32),
        in_specs=[in_vmem, in_vmem, in_vmem, pl.BlockSpec(memory_space=pl.ANY)],
        out_specs=in_vmem,
        scratch_shapes=[
            *[vector((rows, width), jnp.float32) for _ in range(tables)],
            vector((chunks, groups, cap, width), jnp.float32),
            vector((chunks, groups, 2, cap, width), jnp.float32),
            *[vector((chunks, groups, bags, width), jnp.float32) for _ in range(3)],
            vector((slots, tables, bags, 2 * cap), jnp.bfloat16),
            vector((slots, held_rows, 128), jnp.int32),
            pltpu.SMEM((slots, held_rows, 128), jnp.int32),
            vector((look, look), jnp.bfloat16),
            vector((bags, bags), jnp.bfloat16),
            vector((bags, bags), jnp.bfloat16),
            *[dma((chunks, groups)) for _ in range(5)],
            dma((tables, groups)),
            dma((tables, groups)),
            dma((tables,)),
            dma((tables,)),
            dma((slots,)),
        ],
        compiler_params=pltpu.CompilerParams(collective_id=0, has_side_effects=True, vmem_limit_bytes=63 * 2**20),
    )(
        row_shard.reshape(tables * strips, lanes),
        row_offset.reshape(tables, strips, lanes).swapaxes(0, 1).reshape(strips * tables, lanes),
        bag_lengths.reshape(tables * blocks, bags),
        table,
    )


def solution(mesh):
    placed = (P("grp", "row", None), P("grp", None, None), P("grp", None), P("grp", None, None))
    return jax.shard_map(
        body, mesh=mesh, in_specs=placed, out_specs=P(None, ("grp", "row"), None), check_vma=False
    )
```

```python
import functools
import jax
import jax.numpy as jnp
from jax import lax
from jax.experimental import pallas as pl
from jax.experimental.pallas import tpu as pltpu
from jax.sharding import PartitionSpec as P

MESH = pl.DeviceIdType.MESH


def kernel(dims, shard_ref, offset_ref, length_ref, table_hbm, out_ref, *scratch):
    tables, groups, shards, cap, bags, look = dims
    held = scratch[:tables]
    (ysend, comb, part, fromleft, fromright, weights_of, staged, off_ref, earlier, starts_of, ends_of,
     ys_sem, yr_sem, zs_sem, lr_sem, rr_sem, fs_sem, fr_sem, own_sem, tab_sem, off_sem) = scratch[tables:]
    lanes = shard_ref.shape[1]
    halves = look // lanes
    blocks = groups * shards
    slots = weights_of.shape[0]
    line = shards // 2
    chips = groups // 2
    pieces = line * groups
    ahead = weights_of.shape[0] - 3
    g = lax.axis_index("grp")
    r = lax.axis_index("row")
    q = r // 2
    p = r % 2
    mate = q * 2 + 1 - p

    loads = [pltpu.make_async_copy(table_hbm.at[t], held[t], tab_sem.at[t]) for t in range(tables)]
    for load in loads:
        load.start()

    barrier = pltpu.get_barrier_semaphore()
    pl.semaphore_signal(barrier, inc=1, device_id=(g, mate), device_id_type=MESH)

    @pl.when(q > 0)
    def _():
        pl.semaphore_signal(barrier, inc=1, device_id=(g, r - 2), device_id_type=MESH)

    @pl.when(q < line - 1)
    def _():
        pl.semaphore_signal(barrier, inc=1, device_id=(g, r + 2), device_id_type=MESH)

    for step in range(1, groups):
        pl.semaphore_signal(barrier, inc=1, device_id=((g + step) % groups, r), device_id_type=MESH)

    def ones_where(keep):
        return jnp.where(keep, 1.0, 0.0).astype(jnp.bfloat16)

    def grid_of(size):
        return [lax.broadcasted_iota(jnp.int32, (size, size), axis) for axis in range(2)]

    down, across = grid_of(look)
    earlier[...] = ones_where(down < across)
    down, across = grid_of(bags)
    starts_of[...] = ones_where(across < down)
    ends_of[...] = ones_where(across <= down)

    def target(j):
        picked = 0
        for at in range(line):
            order = sorted(range(line), key=lambda d: (-abs(d - at), d))
            for i in range(line):
                picked = picked + jnp.where(jnp.logical_and(q == at, j == i), order[i], 0)
        return picked

    def peer(s):
        return (g // 2 + s // 2) % chips * 2 + (g % 2 + s % 2) % 2

    def origin(s):
        return (g // 2 + chips - s // 2) % chips * 2 + (g % 2 + s % 2) % 2

    def place(n):
        to = target(n // groups)
        s = groups - 1 - n % groups
        return to, s, peer(s)

    def ycopy(c, k):
        return pltpu.make_async_remote_copy(
            src_ref=ysend.at[c, k], dst_ref=comb.at[c, k, 1], send_sem=ys_sem.at[c, k], recv_sem=yr_sem.at[c, k],
            device_id=(g, mate), device_id_type=MESH)

    def rightcopy(c, k):
        return pltpu.make_async_remote_copy(
            src_ref=part.at[c, k], dst_ref=fromleft.at[c, k], send_sem=zs_sem.at[c, k], recv_sem=lr_sem.at[c, k],
            device_id=(g, r + 2), device_id_type=MESH)

    def leftcopy(c, k):
        return pltpu.make_async_remote_copy(
            src_ref=part.at[c, k], dst_ref=fromright.at[c, k], send_sem=zs_sem.at[c, k], recv_sem=rr_sem.at[c, k],
            device_id=(g, r - 2), device_id_type=MESH)

    def ownercopy(c, t, s, k, home):
        return pltpu.make_async_remote_copy(
            src_ref=part.at[c, k], dst_ref=out_ref.at[home * tables + t], send_sem=fs_sem.at[t, s],
            recv_sem=fr_sem.at[t, s], device_id=(k, r), device_id_type=MESH)

    def homecopy(c, t):
        return pltpu.make_async_copy(part.at[c, g], out_ref.at[g * tables + t], own_sem.at[t])

    def across_lanes(a, b):
        return lax.dot_general(a, b, (((1,), (1,)), ((), ())), preferred_element_type=jnp.float32)

    def shards_at(t, o):
        return jnp.concatenate([shard_ref[pl.ds((t * blocks + o) * halves + h, 1), :] for h in range(halves)], axis=1)

    def offsets_at(t, o):
        return jnp.concatenate([offset_ref[pl.ds((o * halves + h) * tables + t, 1), :] for h in range(halves)], axis=1)

    def prepare(n):
        to, s, k = place(n)
        slot = n % slots
        away, here = (k * line + to) * 2 + 1 - p, (k * line + to) * 2 + p
        local = []
        for t in range(tables):
            local.append(jnp.where(shards_at(t, away) == r, 1.0, 0.0))
            local.append(jnp.where(shards_at(t, here) == r, 1.0, 0.0))
            local.append(jnp.where(shards_at(t, here) == mate, 1.0, 0.0))
        local += [jnp.zeros_like(local[0])] * (-len(local) % 8)
        local = jnp.concatenate(local, axis=0)
        rank = jnp.dot(local.astype(jnp.bfloat16), earlier[...], preferred_element_type=jnp.float32)
        rank = jnp.where(local > 0.5, rank, -1.0).astype(jnp.int32)
        slot_ids = lax.broadcasted_iota(jnp.int32, (cap, look), 0)
        places = lax.broadcasted_iota(jnp.int32, (bags, look), 1).astype(jnp.float32)
        for t in range(tables):
            sent, kept, given = [ones_where(rank[3 * t + i:3 * t + i + 1, :] == slot_ids) for i in range(3)]
            for i, (o, chosen) in enumerate(((away, sent), (here, kept))):
                wanted = offsets_at(t, o)
                digits = [wanted // 128, wanted % 128] + [jnp.zeros_like(wanted)] * 6
                digits = jnp.concatenate(digits, axis=0).astype(jnp.float32).astype(jnp.bfloat16)
                packed = across_lanes(digits, chosen)
                index = packed[0:1, :] * 128.0 + packed[1:2, :]
                index = jnp.clip(index.astype(jnp.int32), 0, held[t].shape[0] - 1)
                staged[slot, pl.ds(2 * t + i, 1), pl.ds(0, cap)] = index
            lengths = length_ref[pl.ds(t * blocks + here, 1), :].astype(jnp.float32)
            lengths = jnp.broadcast_to(lengths, (8, bags)).astype(jnp.bfloat16)
            starts = across_lanes(starts_of[...], lengths)[:, 0:1]
            ends = across_lanes(ends_of[...], lengths)[:, 0:1]
            member = ones_where(jnp.logical_and(places >= starts, places < ends))
            weights = across_lanes(member, jnp.concatenate([kept, given], axis=0))
            weights_of[slot, t] = weights.astype(jnp.bfloat16)

    def toscalars(n):
        slot = n % slots
        return pltpu.make_async_copy(staged.at[slot], off_ref.at[slot], off_sem.at[slot])

    def gather(slot, t, i, dst):
        @pl.loop(0, cap // 8)
        def _(b):
            for u in range(8):
                row = off_ref[slot, 2 * t + i, b * 8 + u]
                dst[pl.ds(b * 8 + u, 1), :] = held[t][pl.ds(row, 1), :]

    def fetch(n, first=False):
        to, s, k = place(n)
        slot = n % slots
        toscalars(n).wait()
        for t in range(tables):
            c = to * tables + t
            if first:
                loads[t].wait()
            gather(slot, t, 0, ysend.at[c, k])
            ycopy(c, k).start()
        for t in range(tables):
            gather(slot, t, 1, comb.at[to * tables + t, k, 0])

    def merge(n):
        to, s, k = place(n)
        sums = []
        for t in range(tables):
            c = to * tables + t
            ycopy(c, k).wait_recv()
            weights = weights_of[n % slots, t]
            vectors = jnp.concatenate([comb[c, k, 0], comb[c, k, 1]], axis=0)
            high = vectors.astype(jnp.bfloat16)
            low = (vectors - high.astype(jnp.float32)).astype(jnp.bfloat16)
            sums.append(jnp.dot(weights, high, preferred_element_type=jnp.float32)
                        + jnp.dot(weights, low, preferred_element_type=jnp.float32))
        for t in range(tables):
            c = to * tables + t
            part[c, k] = sums[t]
        for t in range(tables):
            c = to * tables + t

            @pl.when(jnp.logical_and(to >= q, q > 0))
            def _():
                rightcopy(c, k).wait_recv()
                part[c, k] = part[c, k] + fromleft[c, k]

            @pl.when(jnp.logical_and(to <= q, q < line - 1))
            def _():
                leftcopy(c, k).wait_recv()
                part[c, k] = part[c, k] + fromright[c, k]

            @pl.when(to > q)
            def _():
                rightcopy(c, k).start()

            @pl.when(to < q)
            def _():
                leftcopy(c, k).start()

            @pl.when(jnp.logical_and(to == q, s > 0))
            def _():
                ownercopy(c, t, s, k, g).start()

            @pl.when(jnp.logical_and(to == q, s == 0))
            def _():
                homecopy(c, t).start()

    prepare(0)
    prepare(1)
    toscalars(0).start()
    pl.semaphore_wait(barrier, groups + jnp.where(q > 0, 1, 0) + jnp.where(q < line - 1, 1, 0))

    fetch(0, True)
    toscalars(1).start()
    prepare(2)

    @pl.loop(3, pieces + ahead + 2)
    def _(m):
        @pl.when(m - 2 < pieces)
        def _():
            fetch(m - 2)

        @pl.when(m - 1 < pieces)
        def _():
            toscalars(m - 1).start()

        @pl.when(m - 2 - ahead >= 0)
        def _():
            merge(m - 2 - ahead)

        @pl.when(m < pieces)
        def _():
            prepare(m)

    @pl.loop(0, pieces)
    def _(n):
        to, s, k = place(n)
        for t in range(tables):
            c = to * tables + t
            ycopy(c, k).wait_send()

            @pl.when(to != q)
            def _():
                rightcopy(c, k).wait_send()

    @pl.loop(1, groups)
    def _(s):
        for t in range(tables):
            c = q * tables + t
            ownercopy(c, t, s, peer(s), g).wait_send()
            ownercopy(c, t, s, origin(s), origin(s)).wait_recv()

    for t in range(tables):
        homecopy(q * tables + t, t).wait()


def body(table, row_shard, row_offset, bag_lengths):
    groups = lax.axis_size("grp")
    shards = lax.axis_size("row")
    line = shards // 2
    tables, rows, width = table.shape
    bags = bag_lengths.shape[2]
    blocks = groups * shards
    look = row_offset.shape[1] // blocks
    cap = 3 * look // shards
    lanes = min(look, 128)
    strips = row_offset.shape[1] // lanes
    chunks = line * tables
    slots = 5
    held_rows = -(-2 * tables // 8) * 8
    dims = (tables, groups, shards, cap, bags, look)
    vector, dma = pltpu.VMEM, pltpu.SemaphoreType.DMA
    in_vmem = pl.BlockSpec(memory_space=pltpu.VMEM)
    return pl.pallas_call(
        functools.partial(kernel, dims),
        out_shape=jax.ShapeDtypeStruct((groups * tables, bags, width), jnp.float32),
        in_specs=[in_vmem, in_vmem, in_vmem, pl.BlockSpec(memory_space=pl.ANY)],
        out_specs=in_vmem,
        scratch_shapes=[
            *[vector((rows, width), jnp.float32) for _ in range(tables)],
            vector((chunks, groups, cap, width), jnp.float32),
            vector((chunks, groups, 2, cap, width), jnp.float32),
            *[vector((chunks, groups, bags, width), jnp.float32) for _ in range(3)],
            vector((slots, tables, bags, 2 * cap), jnp.bfloat16),
            vector((slots, held_rows, 128), jnp.int32),
            pltpu.SMEM((slots, held_rows, 128), jnp.int32),
            vector((look, look), jnp.bfloat16),
            vector((bags, bags), jnp.bfloat16),
            vector((bags, bags), jnp.bfloat16),
            *[dma((chunks, groups)) for _ in range(5)],
            dma((tables, groups)),
            dma((tables, groups)),
            dma((tables,)),
            dma((tables,)),
            dma((slots,)),
        ],
        compiler_params=pltpu.CompilerParams(collective_id=0, has_side_effects=True, vmem_limit_bytes=63 * 2**20),
    )(
        row_shard.reshape(tables * strips, lanes),
        row_offset.reshape(tables, strips, lanes).swapaxes(0, 1).reshape(strips * tables, lanes),
        bag_lengths.reshape(tables * blocks, bags),
        table,
    )


def solution(mesh):
    placed = (P("grp", "row", None), P("grp", None, None), P("grp", None), P("grp", None, None))
    return jax.shard_map(
        body, mesh=mesh, in_specs=placed, out_specs=P(None, ("grp", "row"), None), check_vma=False
    )
```

```python
import functools
import jax
import jax.numpy as jnp
from jax import lax
from jax.experimental import pallas as pl
from jax.experimental.pallas import tpu as pltpu
from jax.sharding import PartitionSpec as P

MESH = pl.DeviceIdType.MESH


def kernel(dims, shard_ref, offset_ref, length_ref, table_hbm, out_ref, *scratch):
    tables, groups, shards, cap, bags, look = dims
    held = scratch[:tables]
    (ysend, comb, part, fromleft, fromright, weights_of, staged, off_ref, earlier, starts_of, ends_of,
     ys_sem, yr_sem, zs_sem, lr_sem, rr_sem, fs_sem, fr_sem, own_sem, tab_sem, off_sem) = scratch[tables:]
    lanes = shard_ref.shape[1]
    halves = look // lanes
    blocks = groups * shards
    slots = weights_of.shape[0]
    line = shards // 2
    chips = groups // 2
    pieces = line * groups
    ahead = weights_of.shape[0] - 3
    g = lax.axis_index("grp")
    r = lax.axis_index("row")
    q = r // 2
    p = r % 2
    mate = q * 2 + 1 - p

    loads = [pltpu.make_async_copy(table_hbm.at[t], held[t], tab_sem.at[t]) for t in range(tables)]
    for load in loads:
        load.start()

    barrier = pltpu.get_barrier_semaphore()
    pl.semaphore_signal(barrier, inc=1, device_id=(g, mate), device_id_type=MESH)

    @pl.when(q > 0)
    def _():
        pl.semaphore_signal(barrier, inc=1, device_id=(g, r - 2), device_id_type=MESH)

    @pl.when(q < line - 1)
    def _():
        pl.semaphore_signal(barrier, inc=1, device_id=(g, r + 2), device_id_type=MESH)

    for step in range(1, groups):
        pl.semaphore_signal(barrier, inc=1, device_id=((g + step) % groups, r), device_id_type=MESH)

    def ones_where(keep):
        return jnp.where(keep, 1.0, 0.0).astype(jnp.bfloat16)

    def grid_of(size):
        return [lax.broadcasted_iota(jnp.int32, (size, size), axis) for axis in range(2)]

    down, across = grid_of(look)
    earlier[...] = ones_where(down < across)
    down, across = grid_of(bags)
    starts_of[...] = ones_where(across < down)
    ends_of[...] = ones_where(across <= down)

    def target(j):
        picked = 0
        for at in range(line):
            order = sorted(range(line), key=lambda d: (-abs(d - at), d))
            for i in range(line):
                picked = picked + jnp.where(jnp.logical_and(q == at, j == i), order[i], 0)
        return picked

    def peer(s):
        return (g // 2 + s // 2) % chips * 2 + (g % 2 + s % 2) % 2

    def origin(s):
        return (g // 2 + chips - s // 2) % chips * 2 + (g % 2 + s % 2) % 2

    def place(n):
        to = target(n // groups)
        s = groups - 1 - n % groups
        return to, s, peer(s)

    def ycopy(c, k):
        return pltpu.make_async_remote_copy(
            src_ref=ysend.at[c, k], dst_ref=comb.at[c, k, 1], send_sem=ys_sem.at[c, k], recv_sem=yr_sem.at[c, k],
            device_id=(g, mate), device_id_type=MESH)

    def rightcopy(c, k):
        return pltpu.make_async_remote_copy(
            src_ref=part.at[c, k], dst_ref=fromleft.at[c, k], send_sem=zs_sem.at[c, k], recv_sem=lr_sem.at[c, k],
            device_id=(g, r + 2), device_id_type=MESH)

    def leftcopy(c, k):
        return pltpu.make_async_remote_copy(
            src_ref=part.at[c, k], dst_ref=fromright.at[c, k], send_sem=zs_sem.at[c, k], recv_sem=rr_sem.at[c, k],
            device_id=(g, r - 2), device_id_type=MESH)

    def ownercopy(c, t, s, k, home):
        return pltpu.make_async_remote_copy(
            src_ref=part.at[c, k], dst_ref=out_ref.at[home * tables + t], send_sem=fs_sem.at[t, s],
            recv_sem=fr_sem.at[t, s], device_id=(k, r), device_id_type=MESH)

    def homecopy(c, t):
        return pltpu.make_async_copy(part.at[c, g], out_ref.at[g * tables + t], own_sem.at[t])

    def across_lanes(a, b):
        return lax.dot_general(a, b, (((1,), (1,)), ((), ())), preferred_element_type=jnp.float32)

    def shards_at(t, o):
        return jnp.concatenate([shard_ref[pl.ds((t * blocks + o) * halves + h, 1), :] for h in range(halves)], axis=1)

    def offsets_at(t, o):
        return jnp.concatenate([offset_ref[pl.ds((o * halves + h) * tables + t, 1), :] for h in range(halves)], axis=1)

    def prepare(n):
        to, s, k = place(n)
        slot = n % slots
        away, here = (k * line + to) * 2 + 1 - p, (k * line + to) * 2 + p
        local = []
        for t in range(tables):
            local.append(jnp.where(shards_at(t, away) == r, 1.0, 0.0))
            local.append(jnp.where(shards_at(t, here) == r, 1.0, 0.0))
            local.append(jnp.where(shards_at(t, here) == mate, 1.0, 0.0))
        local += [jnp.zeros_like(local[0])] * (-len(local) % 8)
        local = jnp.concatenate(local, axis=0)
        rank = jnp.dot(local.astype(jnp.bfloat16), earlier[...], preferred_element_type=jnp.float32)
        rank = jnp.where(local > 0.5, rank, -1.0).astype(jnp.int32)
        slot_ids = lax.broadcasted_iota(jnp.int32, (cap, look), 0)
        places = lax.broadcasted_iota(jnp.int32, (bags, look), 1).astype(jnp.float32)
        for t in range(tables):
            sent, kept, given = [ones_where(rank[3 * t + i:3 * t + i + 1, :] == slot_ids) for i in range(3)]
            for i, (o, chosen) in enumerate(((away, sent), (here, kept))):
                wanted = offsets_at(t, o)
                digits = [wanted // 128, wanted % 128] + [jnp.zeros_like(wanted)] * 6
                digits = jnp.concatenate(digits, axis=0).astype(jnp.float32).astype(jnp.bfloat16)
                packed = across_lanes(digits, chosen)
                index = packed[0:1, :] * 128.0 + packed[1:2, :]
                index = jnp.clip(index.astype(jnp.int32), 0, held[t].shape[0] - 1)
                staged[slot, pl.ds(2 * t + i, 1), pl.ds(0, cap)] = index
            lengths = length_ref[pl.ds(t * blocks + here, 1), :].astype(jnp.float32)
            lengths = jnp.broadcast_to(lengths, (8, bags)).astype(jnp.bfloat16)
            starts = across_lanes(starts_of[...], lengths)[:, 0:1]
            ends = across_lanes(ends_of[...], lengths)[:, 0:1]
            member = ones_where(jnp.logical_and(places >= starts, places < ends))
            weights = across_lanes(member, jnp.concatenate([kept, given], axis=0))
            weights_of[slot, t] = weights.astype(jnp.bfloat16)

    def toscalars(n):
        slot = n % slots
        return pltpu.make_async_copy(staged.at[slot], off_ref.at[slot], off_sem.at[slot])

    def gather(slot, t, i, dst):
        @pl.loop(0, cap // 8)
        def _(b):
            for u in range(8):
                row = off_ref[slot, 2 * t + i, b * 8 + u]
                dst[pl.ds(b * 8 + u, 1), :] = held[t][pl.ds(row, 1), :]

    def fetch(n, first=False):
        to, s, k = place(n)
        slot = n % slots
        toscalars(n).wait()
        for t in range(tables):
            c = to * tables + t
            if first:
                loads[t].wait()
            gather(slot, t, 0, ysend.at[c, k])
            ycopy(c, k).start()
        for t in range(tables):
            gather(slot, t, 1, comb.at[to * tables + t, k, 0])

    def merge(n):
        to, s, k = place(n)
        sums = []
        for t in range(tables):
            c = to * tables + t
            ycopy(c, k).wait_recv()
            weights = weights_of[n % slots, t]
            vectors = jnp.concatenate([comb[c, k, 0], comb[c, k, 1]], axis=0)
            high = vectors.astype(jnp.bfloat16)
            low = (vectors - high.astype(jnp.float32)).astype(jnp.bfloat16)
            sums.append(jnp.dot(weights, high, preferred_element_type=jnp.float32)
                        + jnp.dot(weights, low, preferred_element_type=jnp.float32))
        for t in range(tables):
            c = to * tables + t
            part[c, k] = sums[t]
        for t in range(tables):
            c = to * tables + t

            @pl.when(jnp.logical_and(to >= q, q > 0))
            def _():
                rightcopy(c, k).wait_recv()
                part[c, k] = part[c, k] + fromleft[c, k]

            @pl.when(jnp.logical_and(to <= q, q < line - 1))
            def _():
                leftcopy(c, k).wait_recv()
                part[c, k] = part[c, k] + fromright[c, k]

            @pl.when(to > q)
            def _():
                rightcopy(c, k).start()

            @pl.when(to < q)
            def _():
                leftcopy(c, k).start()

            @pl.when(jnp.logical_and(to == q, s > 0))
            def _():
                ownercopy(c, t, s, k, g).start()

            @pl.when(jnp.logical_and(to == q, s == 0))
            def _():
                homecopy(c, t).start()

    prepare(0)
    prepare(1)
    toscalars(0).start()
    pl.semaphore_wait(barrier, groups + jnp.where(q > 0, 1, 0) + jnp.where(q < line - 1, 1, 0))

    def advance(m, first=False):
        fetch(m, first)

        @pl.when(m + 1 < pieces)
        def _():
            toscalars(m + 1).start()

        @pl.when(m + 2 < pieces)
        def _():
            prepare(m + 2)

    advance(0, True)
    advance(1)
    merge(0)

    @pl.loop(1, ahead)
    def _(n):
        @pl.loop(0, 2)
        def _(u):
            advance(2 * n + u)
        merge(n)

    @pl.loop(ahead, pieces - ahead)
    def _(n):
        advance(n + ahead)
        merge(n)

    @pl.loop(pieces - ahead, pieces)
    def _(n):
        merge(n)

    @pl.loop(0, pieces)
    def _(n):
        to, s, k = place(n)
        for t in range(tables):
            c = to * tables + t
            ycopy(c, k).wait_send()

            @pl.when(to != q)
            def _():
                rightcopy(c, k).wait_send()

    @pl.loop(1, groups)
    def _(s):
        for t in range(tables):
            c = q * tables + t
            ownercopy(c, t, s, peer(s), g).wait_send()
            ownercopy(c, t, s, origin(s), origin(s)).wait_recv()

    for t in range(tables):
        homecopy(q * tables + t, t).wait()


def body(table, row_shard, row_offset, bag_lengths):
    groups = lax.axis_size("grp")
    shards = lax.axis_size("row")
    line = shards // 2
    tables, rows, width = table.shape
    bags = bag_lengths.shape[2]
    blocks = groups * shards
    look = row_offset.shape[1] // blocks
    cap = 3 * look // shards
    lanes = min(look, 128)
    strips = row_offset.shape[1] // lanes
    chunks = line * tables
    slots = min(6, line * groups // 2) + 3
    held_rows = -(-2 * tables // 8) * 8
    dims = (tables, groups, shards, cap, bags, look)
    vector, dma = pltpu.VMEM, pltpu.SemaphoreType.DMA
    in_vmem = pl.BlockSpec(memory_space=pltpu.VMEM)
    return pl.pallas_call(
        functools.partial(kernel, dims),
        out_shape=jax.ShapeDtypeStruct((groups * tables, bags, width), jnp.float32),
        in_specs=[in_vmem, in_vmem, in_vmem, pl.BlockSpec(memory_space=pl.ANY)],
        out_specs=in_vmem,
        scratch_shapes=[
            *[vector((rows, width), jnp.float32) for _ in range(tables)],
            vector((chunks, groups, cap, width), jnp.float32),
            vector((chunks, groups, 2, cap, width), jnp.float32),
            *[vector((chunks, groups, bags, width), jnp.float32) for _ in range(3)],
            vector((slots, tables, bags, 2 * cap), jnp.bfloat16),
            vector((slots, held_rows, 128), jnp.int32),
            pltpu.SMEM((slots, held_rows, 128), jnp.int32),
            vector((look, look), jnp.bfloat16),
            vector((bags, bags), jnp.bfloat16),
            vector((bags, bags), jnp.bfloat16),
            *[dma((chunks, groups)) for _ in range(5)],
            dma((tables, groups)),
            dma((tables, groups)),
            dma((tables,)),
            dma((tables,)),
            dma((slots,)),
        ],
        compiler_params=pltpu.CompilerParams(collective_id=0, has_side_effects=True, vmem_limit_bytes=63 * 2**20),
    )(
        row_shard.reshape(tables * strips, lanes),
        row_offset.reshape(tables, strips, lanes).swapaxes(0, 1).reshape(strips * tables, lanes),
        bag_lengths.reshape(tables * blocks, bags),
        table,
    )


def solution(mesh):
    placed = (P("grp", "row", None), P("grp", None, None), P("grp", None), P("grp", None, None))
    return jax.shard_map(
        body, mesh=mesh, in_specs=placed, out_specs=P(None, ("grp", "row"), None), check_vma=False
    )
```
